256 devices in a mesh: gx: 16 (over z_lo, y), gy: 16 (over x, z_hi, core).
Axes of the slice: x: 4, y: 4, z: 8 (z_hi: 2, z_lo: 4; z = z_hi * 4 + z_lo), core: 2. Of those that a mesh axis runs over, the one named last changes fastest.
Arguments:
- position: float32 [3, 4194304], P(None, ('gx', 'gy')), may hold values from -3 to 321.2
- velocity: float32 [3, 4194304], P(None, ('gx', 'gy')), may hold values from -0.6 to 0.6
- mass: float32 [4194304], P(('gx', 'gy')), may hold values from 0.01 to 0.04
- smoothing: float32 [4194304], P(('gx', 'gy')), may hold values from 0.8 to 1.25
- energy: float32 [4194304], P(('gx', 'gy')), may hold values from 0.35 to 5.6
- live_blocks: int32 [256], P(('gx', 'gy')), may hold values from 64 to 128, as said below
- send_list: int32 [256, 18, 12], P(('gx', 'gy')), may hold values from 0 to 23, as said below
- nbr_list: int32 [32768, 8], P(('gx', 'gy')), may hold values from 0 to 343, as said below
- nbr_count: int32 [32768], P(('gx', 'gy')), may hold values from 4 to 8
Outputs:
- density: float32 [4194304], P(('gx', 'gy'))
- kick: float32 [3, 4194304], P(None, ('gx', 'gy'))
- heating: float32 [4194304], P(('gx', 'gy'))
The draws below stay inside these ranges and needn't reach their ends.
Inputs may be any that keep to these rules, and one draw needn't show every extreme that they name: `live_blocks`: the live blocks of a domain are its first ones; some domain has all 128 live and some exactly 64. `send_list`: entries are block indices within the sending domain, all among its first 24 blocks and distinct within one peer list; entry 0 of every list p below 16 is block 0. List p below 16 goes to the domain of fine index p in the same segment, list 16 to the previous segment's domain of the same fine index, list 16 + 1 to the next one's. `nbr_list`: entry 0 of a block's list is the block itself; the others are distinct slots: a live block of the own domain, or a slot 128 + p * 12 + s received from another domain, where p is not the domain's own fine index, p = 16 only if a previous segment exists and p = 17 only if a next one exists.
All inputs are finite; a program needn't handle non-finite values.
Results may differ from the reference program's by a relative error of at most 0.0003.
Values sent between devices are 32-bit elements; how exact they have to be, the bound alone decides.
No kernel may reach another device: no remote copies, remote signals or barrier semaphores. Data moves between devices by JAX's collectives and lax.ppermute only.
A program may use at most 64 MiB of HBM per device.

```python
import math
import jax
import jax.numpy as jnp
from jax import lax

BLOCK = 128
B_DEV = 128
S = 12
NB = 8
SEGMENTS = 16
FINE = 16
DOMAINS = 256
PEERS = 18
SLOTS = 344
BLOCKS = 32768
PARTICLES = 4194304


CELL_SPACING = 1.6


PARTNER_OFFSET = 0.8


BLOCK_SPACING = 2.0


def live_of(key):
    base_key = jax.random.fold_in(key, 101)
    first_key, second_key = jax.random.split(base_key)
    counts = jax.random.randint(first_key, (DOMAINS,), B_DEV // 2, B_DEV + 1, dtype=jnp.int32)
    chosen = jax.random.randint(second_key, (), 0, DOMAINS, dtype=jnp.int32)
    domain_region = jnp.arange(DOMAINS, dtype=jnp.int32)
    counts = jnp.where(domain_region == chosen, B_DEV, counts)
    counts = jnp.where(domain_region == (chosen + 1) % DOMAINS, B_DEV // 2, counts)
    return counts.astype(jnp.int32)


def draw_live_blocks(key, part):
    return live_of(key)


def draw_send_list(key, part):
    counts = live_of(key)
    base_key = jax.random.fold_in(key, 202)
    width_limit = 2 * S
    raw = jax.random.randint(base_key, (DOMAINS, PEERS, width_limit), 0, 4096, dtype=jnp.int32)
    index_value = jnp.arange(width_limit, dtype=jnp.int32)
    score_values = raw * width_limit + index_value[None, None, :]
    full_table = jnp.argmax(counts == B_DEV).astype(jnp.int32)
    domain_region = jnp.arange(DOMAINS, dtype=jnp.int32)[:, None, None]
    peer_domain = jnp.arange(PEERS, dtype=jnp.int32)[None, :, None]
    extra_score = (domain_region == full_table) & (peer_domain == 0) & (index_value[None, None, :] == width_limit - 1) | (domain_region == full_table) & (peer_domain == 1) & (index_value[None, None, :] == 0)
    score_values = score_values + jnp.where(extra_score, 4096 * width_limit, 0)
    first_block = (peer_domain < FINE) & (index_value[None, None, :] == 0)
    score_values = score_values + jnp.where(first_block, 3 * 4096 * width_limit, 0)
    _, picked = lax.top_k(score_values, S)
    return picked.astype(jnp.int32)


def draw_nbr_count(key, part):
    base_key = jax.random.fold_in(key, 303)
    counts = jax.random.randint(base_key, (BLOCKS,), NB // 2, NB + 1, dtype=jnp.int32)
    counts = counts.at[0].set(NB)
    counts = counts.at[1].set(NB // 2)
    return counts.astype(jnp.int32)


def draw_nbr_list(key, part):
    counts = live_of(key)
    sent = draw_send_list(key, part)
    base_key = jax.random.fold_in(key, 404)
    half_fine = max(FINE // 2, 1)
    domain_region = jnp.arange(DOMAINS, dtype=jnp.int32)
    segment = domain_region // FINE
    fine_index = domain_region % FINE
    src_fine = segment[:, None] * FINE + jnp.arange(FINE, dtype=jnp.int32)[None, :]
    ghost_fine = sent[src_fine, fine_index[:, None]].reshape(DOMAINS, FINE * S)
    ghost_lower = sent[jnp.maximum(domain_region - FINE, 0), FINE + 1]
    ghost_upper = sent[jnp.minimum(domain_region + FINE, DOMAINS - 1), FINE]
    ghost_block = jnp.concatenate([ghost_fine, ghost_lower, ghost_upper], axis=1)
    slot = jnp.arange(SLOTS, dtype=jnp.int32)[None, None, :]
    block = jnp.arange(B_DEV, dtype=jnp.int32)[None, :, None]
    peer_domain = (slot - B_DEV) // S
    seg3 = segment[:, None, None]
    fine3 = fine_index[:, None, None]
    local_ok = (slot < counts[:, None, None]) & (slot != block)
    ghost_ok = (peer_domain < FINE) & (peer_domain != fine3) | (peer_domain == FINE) & (seg3 > 0) | (peer_domain == FINE + 1) & (seg3 < SEGMENTS - 1)
    allowed = jnp.where(slot < B_DEV, local_ok, ghost_ok)
    ghost_index = jnp.clip(slot - B_DEV, 0, PEERS * S - 1)
    source_block = jnp.take_along_axis(jnp.broadcast_to(ghost_block[:, None, :], (DOMAINS, 1, PEERS * S)), jnp.broadcast_to(ghost_index, (1, 1, SLOTS)) * jnp.ones((DOMAINS, 1, 1), jnp.int32), axis=2)
    lateral = jnp.abs(jnp.where(peer_domain < FINE, peer_domain % half_fine - fine3 % half_fine, 0))
    local_near = jnp.abs(slot - block) <= 3
    ghost_near = (jnp.abs(source_block - block) <= 2) & (lateral <= 2)
    near = jnp.where(slot < B_DEV, local_near, ghost_near)
    raw = jax.random.randint(base_key, (DOMAINS, B_DEV, SLOTS), 0, 4096, dtype=jnp.int32)
    score_values = raw * SLOTS + slot + jnp.where(near, 4096 * SLOTS, 0)
    forced = (domain_region[:, None, None] == 0) & (block == 0) & (slot == SLOTS - 1)
    partner = (fine3 + half_fine) % FINE
    partner_slot = (block == 0) & (slot == B_DEV + partner * S)
    forced = forced | partner_slot
    score_values = score_values + jnp.where(forced, 2 * 4096 * SLOTS, 0)
    score_values = jnp.where(allowed, score_values, -1)
    _, picked = lax.top_k(score_values, NB - 1)
    itself = jnp.broadcast_to(jnp.arange(B_DEV, dtype=jnp.int32)[None, :, None], (DOMAINS, B_DEV, 1))
    return jnp.concatenate([itself, picked.astype(jnp.int32)], axis=2).reshape(BLOCKS, NB).astype(jnp.int32)


def draw_position(key, part):
    base_key = jax.random.fold_in(key, 606)
    side_key, along_key = jax.random.split(base_key)
    half_fine = max(FINE // 2, 1)
    block = jnp.arange(BLOCKS, dtype=jnp.int32)
    domain_region = block // B_DEV
    inner = block % B_DEV
    segment = domain_region // FINE
    fine_index = domain_region % FINE
    centre_x = (fine_index % half_fine).astype(jnp.float32) * CELL_SPACING
    centre_y = (2 * segment).astype(jnp.float32) * CELL_SPACING + (fine_index // half_fine).astype(jnp.float32) * PARTNER_OFFSET
    centre_z = inner.astype(jnp.float32) * BLOCK_SPACING
    centre = jnp.stack([centre_x, centre_y, centre_z])
    sideways = jnp.clip(0.7 * jax.random.normal(side_key, (2, BLOCKS, BLOCK), jnp.float32), -2.1, 2.1)
    along = jnp.clip(jax.random.normal(along_key, (1, BLOCKS, BLOCK), jnp.float32), -3.0, 3.0)
    spread = jnp.concatenate([sideways, along], axis=0)
    return (centre[:, :, None] + spread).reshape(3, PARTICLES)


def draw_energy(key, part):
    base_key = jax.random.fold_in(key, 505)
    first_key, second_key = jax.random.split(base_key)
    factor = jnp.exp(jax.random.uniform(first_key, (DOMAINS, 1), jnp.float32, math.log(0.5), math.log(4.0)))
    spread = jnp.exp(jax.random.uniform(second_key, (DOMAINS, B_DEV * BLOCK), jnp.float32, math.log(0.7), math.log(1.4)))
    return (factor * spread).reshape(PARTICLES)


def steps_of(key, shape, cuts, least, high):
    gain = 1.0
    for axis_at, blocks in cuts:
        heights = jax.random.uniform(jax.random.fold_in(jax.random.fold_in(key, 6), axis_at), (blocks,), jnp.float32, least / len(cuts), high / len(cuts))
        gain = gain * jnp.repeat(jnp.exp(heights), shape[axis_at] // blocks).reshape((-1,) + (1,) * (len(shape) - 1 - axis_at))
    return gain


def bell_draw(key, dims, scale, bound, cuts=(), held_as=jnp.bfloat16):
    loudness = steps_of(key, dims, cuts, -0.22, 0.18) if cuts else 1.0
    result = jax.random.normal(key, dims, jnp.float32) * scale * loudness
    return jnp.minimum(jnp.maximum(result, -bound), bound).astype(held_as)


def setup_inputs(seed: int = 0) -> dict:
    streams_of = jax.random.split(jax.random.key(seed), 10)
    position = draw_position(jax.random.fold_in(streams_of[9], 71), 0)
    velocity = bell_draw(streams_of[1], (3, PARTICLES), 0.1, 0.6, ((1, 256),), jnp.float32)
    mass = jnp.clip(jnp.exp(math.log(0.04) - 1.3862944 * jax.random.uniform(streams_of[2], (PARTICLES,), jnp.float32) ** steps_of(streams_of[2], (PARTICLES,), ((0, 256),), -0.2, 0.2)), 0.01, 0.04)
    smoothing = jnp.clip(jnp.exp(math.log(1.25) - 0.4462871 * jax.random.uniform(streams_of[3], (PARTICLES,), jnp.float32) ** steps_of(streams_of[3], (PARTICLES,), ((0, 256),), -0.2, 0.2)), 0.8, 1.25)
    energy = draw_energy(jax.random.fold_in(streams_of[9], 71), 0)
    live_blocks = draw_live_blocks(jax.random.fold_in(streams_of[9], 71), 0)
    send_list = draw_send_list(jax.random.fold_in(streams_of[9], 71), 0)
    nbr_list = draw_nbr_list(jax.random.fold_in(streams_of[9], 71), 0)
    nbr_count = draw_nbr_count(jax.random.fold_in(streams_of[9], 71), 0)
    return dict(position=position, velocity=velocity, mass=mass, smoothing=smoothing, energy=energy, live_blocks=live_blocks, send_list=send_list, nbr_list=nbr_list, nbr_count=nbr_count)


GAMMA = 5.0 / 3.0
VISC_ALPHA = 1.0
VISC_BETA = 2.0
ETA_SQUARED = 0.01
COURANT = 0.3
KERNEL_NORM = 21.0 / (16.0 * math.pi)
FAR_STEP = 1e+30

def kernel_sum(target_pos, target_smooth, source_pos, source_weight):
    squares = sum(((target_pos[component][:, None, :] - source_pos[component][:, :, None]) ** 2 for component in range(3)))
    ratio = jnp.sqrt(squares) / target_smooth[:, None, :]
    taper = jnp.maximum(1.0 - 0.5 * ratio, 0.0)
    profile = taper ** 4 * (1.0 + 2.0 * ratio)
    total = lax.optimization_barrier(jnp.sum(source_weight[:, :, None] * profile, axis=1))
    return KERNEL_NORM / target_smooth ** 3 * total

def pressure_terms(dens, thermal):
    return ((GAMMA - 1.0) * thermal / dens, jnp.sqrt(GAMMA * (GAMMA - 1.0) * thermal))

def force_sum(target, source, source_weight, source_valid):
    target_pos, target_vel, target_smooth, target_dens, target_press, target_sound = target
    source_pos, source_vel, source_smooth, source_dens, source_press, source_sound = source
    offsets = [target_pos[component][:, None, :] - source_pos[component][:, :, None] for component in range(3)]
    moving = [target_vel[component][:, None, :] - source_vel[component][:, :, None] for component in range(3)]
    squares = offsets[0] * offsets[0] + offsets[1] * offsets[1] + offsets[2] * offsets[2]
    closing = offsets[0] * moving[0] + offsets[1] * moving[1] + offsets[2] * moving[2]
    mean_smooth = 0.5 * (target_smooth[:, None, :] + source_smooth[:, :, None])
    taper = jnp.maximum(1.0 - 0.5 * jnp.sqrt(squares) / mean_smooth, 0.0)
    slope = -5.0 * KERNEL_NORM * taper ** 3 / mean_smooth ** 5
    approach = mean_smooth * jnp.minimum(closing, 0.0) / (squares + ETA_SQUARED * mean_smooth * mean_smooth)
    mean_sound = 0.5 * (target_sound[:, None, :] + source_sound[:, :, None])
    mean_dens = 0.5 * (target_dens[:, None, :] + source_dens[:, :, None])
    visc = (-VISC_ALPHA * mean_sound * approach + VISC_BETA * approach * approach) / mean_dens
    coef = source_weight[:, :, None] * (target_press[:, None, :] + source_press[:, :, None] + visc) * slope
    accel = jnp.stack([-lax.optimization_barrier(jnp.sum(coef * offset, axis=1)) for offset in offsets])
    rate = 0.5 * lax.optimization_barrier(jnp.sum(coef * closing, axis=1))
    signal = lax.optimization_barrier(jnp.max(jnp.where(source_valid[:, :, None], -approach, 0.0), axis=1))
    return (accel, rate, signal)

def reference(position, velocity, mass, smoothing, energy, live_blocks, send_list, nbr_list, nbr_count):
    domain_region = jnp.arange(DOMAINS, dtype=jnp.int32)
    segment = domain_region // FINE
    fine_index = domain_region % FINE
    peer_ids = jnp.arange(FINE, dtype=jnp.int32)
    src_fine = segment[:, None] * FINE + peer_ids[None, :]
    gid_fine = (src_fine[:, :, None] * B_DEV + send_list[src_fine, fine_index[:, None]]).reshape(DOMAINS, FINE * S)
    src_lower = jnp.maximum(domain_region - FINE, 0)
    gid_lower = src_lower[:, None] * B_DEV + send_list[src_lower, FINE + 1]
    src_upper = jnp.minimum(domain_region + FINE, DOMAINS - 1)
    gid_upper = src_upper[:, None] * B_DEV + send_list[src_upper, FINE]
    gid_own = domain_region[:, None] * B_DEV + jnp.arange(B_DEV, dtype=jnp.int32)[None, :]
    slot_block = jnp.concatenate([gid_own, gid_fine, gid_lower, gid_upper], axis=1).astype(jnp.int32)
    lists = nbr_list.reshape(DOMAINS, B_DEV, NB)
    counts = nbr_count.reshape(DOMAINS, B_DEV)
    usable = jnp.arange(NB, dtype=jnp.int32)[None, None, :] < counts[:, :, None]
    usable = jnp.repeat(usable, BLOCK, axis=2)
    places = position.reshape(3, BLOCKS, BLOCK)
    speeds = velocity.reshape(3, BLOCKS, BLOCK)
    masses = mass.reshape(BLOCKS, BLOCK)
    smooth = smoothing.reshape(BLOCKS, BLOCK)
    thermal = energy.reshape(BLOCKS, BLOCK)

    def density_of(index_value):
        chosen = slot_block[index_value][lists[index_value]]
        source_pos = places[:, chosen].reshape(3, B_DEV, NB * BLOCK)
        weight = jnp.where(usable[index_value], masses[chosen].reshape(B_DEV, NB * BLOCK), 0.0)
        start = (index_value * B_DEV).astype(jnp.int32)
        target_pos = lax.dynamic_slice_in_dim(places, start, B_DEV, 1)
        target_smooth = lax.dynamic_slice_in_dim(smooth, start, B_DEV, 0)
        return kernel_sum(target_pos, target_smooth, source_pos, weight)
    rho = lax.map(density_of, domain_region).reshape(BLOCKS, BLOCK)
    press, sound = pressure_terms(rho, thermal)

    def force_of(index_value):
        chosen = slot_block[index_value][lists[index_value]]
        start = (index_value * B_DEV).astype(jnp.int32)

        def pick(table):
            return table[..., chosen, :].reshape(table.shape[:-2] + (B_DEV, NB * BLOCK))

        def own(table):
            return lax.dynamic_slice_in_dim(table, start, B_DEV, table.ndim - 2)
        weight = jnp.where(usable[index_value], pick(masses), 0.0)
        target = (own(places), own(speeds), own(smooth), own(rho), own(press), own(sound))
        source = (pick(places), pick(speeds), pick(smooth), pick(rho), pick(press), pick(sound))
        return force_sum(target, source, weight, usable[index_value])
    accel, rate, signal = lax.map(force_of, domain_region)
    accel = jnp.moveaxis(accel, 1, 0).reshape(3, PARTICLES)
    rate = rate.reshape(PARTICLES)
    signal = signal.reshape(PARTICLES)
    alive = jnp.arange(B_DEV, dtype=jnp.int32)[None, :, None] < live_blocks[:, None, None]
    alive = jnp.broadcast_to(alive, (DOMAINS, B_DEV, BLOCK)).reshape(PARTICLES)
    sound_flat = sound.reshape(PARTICLES)
    step = COURANT * smoothing / (sound_flat + 1.2 * (VISC_ALPHA * sound_flat + VISC_BETA * signal))
    timestep = jnp.min(jnp.where(alive, step, FAR_STEP))
    density = jnp.where(alive, rho.reshape(PARTICLES), 0.0)
    kick = jnp.where(alive[None, :], timestep * accel, 0.0)
    heating = jnp.where(alive, timestep * rate, 0.0)
    return (density, kick, heating)
```

```python
import math

import jax
import jax.numpy as jnp
from jax import lax
from jax.experimental import pallas as pl
from jax.experimental.pallas import tpu as pltpu
from jax.sharding import PartitionSpec as P

COURANT = 0.3
FAR_STEP = 1e30
TINY = 1e-30
LANES = 128
CHUNK = 8
FIRST = 24
PEER_TILES = 14
PEER_ROWS = 16
F32 = jnp.float32

SMEM = pl.BlockSpec(memory_space=pltpu.SMEM)
VMEM = pl.BlockSpec(memory_space=pltpu.VMEM)


def struct(*shape):
    return jax.ShapeDtypeStruct(shape, F32)


def columns(row):
    return jnp.broadcast_to(row, (LANES, LANES)).T


def spread(row):
    return jnp.broadcast_to(row, (CHUNK, LANES))


def pack_kernel(send, position, velocity, mass, smooth, energy, table, fine, lower, upper):
    blocks = mass.shape[0]

    def build(k, carry):
        at = pl.ds(pl.multiple_of(k * LANES, LANES), LANES)
        row = pl.ds(k, 1)
        table[k] = jnp.concatenate(
            [position[:, at], mass[row, :], -2.0 * velocity[:, at], smooth[row, :]], axis=0
        )
        return carry

    lax.fori_loop(0, blocks, build, 0)

    def fill(target, first_tile, p):
        for s in range(12):
            k = send[p * 12 + s]
            target[first_tile + s] = table[k]
            target[first_tile + 12 + s // 8, s % 8 : s % 8 + 1, :] = energy[pl.ds(k, 1), :]
        target[first_tile + 13, 4:8, :] = jnp.zeros((4, LANES), F32)

    def peer(p, carry):
        fill(fine, p * PEER_TILES, p)
        return carry

    lax.fori_loop(0, 16, peer, 0)
    fill(lower, 0, 16)
    fill(upper, 0, 17)


def density_sum(cols, rows_of, count):
    def one(j, sums):
        xs, ys, zs, ms = rows_of(j)
        out = []
        for c in range(LANES // CHUNK):
            at = pl.ds(c * CHUNK, CHUNK)
            dx = cols[0, at, :] - xs
            dy = cols[1, at, :] - ys
            dz = cols[2, at, :] - zs
            r2 = dx * dx + dy * dy + dz * dz
            u2 = r2 * cols[3, at, :]
            u = u2 * lax.rsqrt(jnp.maximum(u2, TINY))
            t = jnp.maximum(1.0 - u, 0.0)
            t2 = t * t
            out.append(sums[c] + (t2 * ms) * (t2 * (1.25 - t)))
        return tuple(out)

    zero = tuple(jnp.zeros((CHUNK, LANES), F32) for _ in range(LANES // CHUNK))
    sums = lax.fori_loop(0, count, one, zero)
    return jnp.sum(jnp.concatenate(sums, axis=0).T, axis=0, keepdims=True)


def density_columns(cols, table, t):
    for f in range(3):
        cols[f] = columns(table[t, f : f + 1, :])
    h = table[t, 7:8, :]
    cols[3] = columns(0.25 / (h * h))
    return (21.0 / (4.0 * math.pi)) / (h * h * h)


def density_rows(source, tile):
    return [spread(source[tile, f : f + 1, :]) for f in range(4)]


def local_density_kernel(lists, counts, live, table, out, cols):
    out[...] = jnp.zeros_like(out)

    def block(t, carry):
        norm = density_columns(cols, table, t)
        total = density_sum(cols, lambda j: density_rows(table, lists[t * 8 + j]), counts[t])
        out[pl.ds(t, 1), :] = norm * total
        return carry

    lax.fori_loop(0, live[0], block, 0)


def ghost_density(lists, counts, table, ghosts, out, cols, lo, hi):
    def block(t, carry):
        @pl.when(counts[t] > 0)
        def _():
            norm = density_columns(cols, table, t)

            def rows_of(j):
                g = lists[t * 8 + j]
                return density_rows(ghosts, g - 2 * (g // PEER_ROWS))

            total = density_sum(cols, rows_of, counts[t])
            out[pl.ds(t, 1), :] += norm * total

        return carry

    lax.fori_loop(lo, hi, block, 0)


def first_density_kernel(send, lists, counts, table, ghosts, rho, first, fine, lower, upper, cols):
    first[...] = rho[0:FIRST, :]
    ghost_density(lists, counts, table, ghosts, first, cols, 0, FIRST)

    def fill(target, first_row, p):
        for s in range(12):
            target[pl.ds(first_row + s, 1), :] = first[pl.ds(send[p * 12 + s], 1), :]
        for s in range(12, 16):
            target[pl.ds(first_row + s, 1), :] = jnp.zeros((1, LANES), F32)

    def peer(p, carry):
        fill(fine, p * PEER_ROWS, p)
        return carry

    lax.fori_loop(0, 16, peer, 0)
    fill(lower, 0, 16)
    fill(upper, 0, 17)


def rest_density_kernel(
    lists, counts, live, table, ghosts, rho, first, energy, density, state, cols
):
    density[...] = rho[...]
    density[0:FIRST, :] = first[...]
    ghost_density(lists, counts, table, ghosts, density, cols, FIRST, live[0])
    thermal = energy[...]
    dens = density[...]
    state[0] = (2.0 / 3.0) * thermal / dens
    state[1] = jnp.sqrt((10.0 / 9.0) * thermal)
    state[2] = 4.0 * dens


def force_columns(cols, table, state, t):
    for i, f in enumerate((0, 1, 2, 4, 5, 6, 7)):
        cols[i] = columns(table[t, f : f + 1, :])
    for f in range(3):
        cols[7 + f] = columns(state[f, pl.ds(t, 1), :])


def force_one(cols, acc, source, sources_state, tile, row, first):
    xs, ys, zs, ms, us, vs, ws, hs = [spread(source[tile, f : f + 1, :]) for f in range(8)]
    ps, cs, rs = [spread(sources_state[f, pl.ds(row, 1), :]) for f in range(3)]
    for c in range(LANES // CHUNK):
        at = pl.ds(c * CHUNK, CHUNK)
        dx = cols[0, at, :] - xs
        dy = cols[1, at, :] - ys
        dz = cols[2, at, :] - zs
        r2 = dx * dx + dy * dy + dz * dz
        w = dx * (cols[3, at, :] - us) + dy * (cols[4, at, :] - vs) + dz * (cols[5, at, :] - ws)
        q = 1.0 / (cols[6, at, :] + hs)
        q2 = q * q
        u2 = r2 * q2
        u = u2 * lax.rsqrt(jnp.maximum(u2, TINY))
        tq = jnp.maximum(1.0 - u, 0.0) * q
        slope = (tq * tq) * (tq * q2)
        m = (jnp.maximum(w, 0.0) * q) / (u2 + 0.0025)
        visc = m * (cols[8, at, :] + cs + m) / (cols[9, at, :] + rs)
        coef = (slope * ms) * (cols[7, at, :] + ps + visc)
        terms = (coef * dx, coef * dy, coef * dz, coef * w)
        if first:
            for f in range(4):
                acc[f, at, :] = terms[f]
            acc[4, at, :] = m
        else:
            for f in range(4):
                acc[f, at, :] += terms[f]
            acc[4, at, :] = jnp.maximum(acc[4, at, :], m)


def force_totals(acc):
    scale = 210.0 / math.pi
    out = [scale * jnp.sum(acc[f].T, axis=0, keepdims=True) for f in range(3)]
    out.append(0.25 * scale * jnp.sum(acc[3].T, axis=0, keepdims=True))
    out.append(0.25 * jnp.max(acc[4].T, axis=0, keepdims=True))
    return out


def local_force_kernel(lists, counts, live, table, state, out, cols, acc):
    out[...] = jnp.zeros_like(out)

    def block(t, carry):
        force_columns(cols, table, state, t)
        force_one(cols, acc, table, state, t, t, True)

        def step(j, inner):
            s = lists[t * 8 + j]
            force_one(cols, acc, table, state, s, s, False)
            return inner

        lax.fori_loop(1, counts[t], step, 0)
        for f, row in enumerate(force_totals(acc)):
            out[f, pl.ds(t, 1), :] = row
        return carry

    lax.fori_loop(0, live[0], block, 0)


def ghost_force_kernel(
    lists, counts, live, table, state, ghosts, ghost_rho, smooth, local, out, least, ghost_state, cols, acc
):
    out[...] = local[...]
    for p in range(18):
        at = pl.ds(p * PEER_ROWS, PEER_ROWS)
        thermal = ghosts[p * PEER_TILES + 12 : p * PEER_TILES + 14].reshape(PEER_ROWS, LANES)
        dens = ghost_rho[at, :]
        ghost_state[0, at, :] = (2.0 / 3.0) * thermal / dens
        ghost_state[1, at, :] = jnp.sqrt((10.0 / 9.0) * thermal)
        ghost_state[2, at, :] = 4.0 * dens

    def block(t, carry):
        @pl.when(counts[t] > 0)
        def _():
            force_columns(cols, table, state, t)

            def one(j, is_first):
                g = lists[t * 8 + j]
                force_one(
                    cols, acc, ghosts, ghost_state, g - 2 * (g // PEER_ROWS), g, is_first
                )

            one(0, True)

            def step(j, inner):
                one(j, False)
                return inner

            lax.fori_loop(1, counts[t], step, 0)
            rows = force_totals(acc)
            at = pl.ds(t, 1)
            for f in range(4):
                out[f, at, :] += rows[f]
            out[4, at, :] = jnp.maximum(out[4, at, :], rows[4])

        return carry

    lax.fori_loop(0, live[0], block, 0)
    sound = state[1]
    step = COURANT * smooth[...] / (sound + 1.2 * (sound + 2.0 * out[4]))
    index = lax.broadcasted_iota(jnp.int32, step.shape, 0)
    least[0] = jnp.min(jnp.where(index < live[0], step, FAR_STEP))


def scale_kernel(least, forces, kick, heating):
    dt = least[0]

    def block(k, carry):
        row = pl.ds(k, 1)
        at = pl.ds(pl.multiple_of(k * LANES, LANES), LANES)
        for f in range(3):
            kick[f : f + 1, at] = dt * forces[f, row, :]
        return carry

    lax.fori_loop(0, forces.shape[1], block, 0)
    heating[...] = dt * forces[3]


def compacted(values, chosen):
    rank = jnp.sum(
        jnp.tril(jnp.ones((8, 8), jnp.int32), -1)[None] * chosen.astype(jnp.int32)[:, None, :], axis=2
    )
    hit = chosen[:, None, :] & (rank[:, None, :] == jnp.arange(8, dtype=jnp.int32)[None, :, None])
    lists = jnp.sum(jnp.where(hit, values[:, None, :], 0), axis=2)
    return lists.reshape(-1), jnp.sum(chosen.astype(jnp.int32), axis=1)


def shards(
    position, velocity, mass, smoothing, energy, live_blocks, send_list, nbr_list, nbr_count
):
    blocks = nbr_count.shape[0]
    mass2 = mass.reshape(blocks, LANES)
    smooth2 = smoothing.reshape(blocks, LANES)
    energy2 = energy.reshape(blocks, LANES)
    send = send_list.reshape(-1)

    table, fine, lower, upper = pl.pallas_call(
        pack_kernel,
        out_shape=(
            struct(blocks, 8, LANES),
            struct(16 * PEER_TILES, 8, LANES),
            struct(PEER_TILES, 8, LANES),
            struct(PEER_TILES, 8, LANES),
        ),
        in_specs=[SMEM] + [VMEM] * 5,
        out_specs=(VMEM,) * 4,
        name="pack",
    )(send, position, velocity, mass2, smooth2, energy2)

    def exchange(fine, lower, upper):
        shape = (16, fine.shape[0] // 16) + fine.shape[1:]
        arrived = lax.all_to_all(fine.reshape(shape), "gy", split_axis=0, concat_axis=0, tiled=True)
        size = lax.axis_size("gx")
        up = [(i, i + 1) for i in range(size - 1)]
        down = [(j, i) for i, j in up]
        before = lax.ppermute(upper, "gx", up)
        after = lax.ppermute(lower, "gx", down)
        return jnp.concatenate([arrived.reshape(fine.shape), before, after], axis=0)

    ghosts = exchange(fine, lower, upper)

    used = jnp.arange(8, dtype=jnp.int32)[None, :] < nbr_count[:, None]
    is_local = nbr_list < blocks
    local_lists, local_counts = compacted(nbr_list, used & is_local)
    slot = nbr_list - blocks
    ghost_lists, ghost_counts = compacted(slot + 4 * (slot // 12), used & ~is_local)

    cols4 = pltpu.VMEM((4, LANES, LANES), F32)
    local_rho = pl.pallas_call(
        local_density_kernel,
        out_shape=struct(blocks, LANES),
        in_specs=[SMEM] * 3 + [VMEM],
        out_specs=VMEM,
        scratch_shapes=[cols4],
        name="local_density",
    )(local_lists, local_counts, live_blocks, table)

    first, fine_rho, lower_rho, upper_rho = pl.pallas_call(
        first_density_kernel,
        out_shape=(
            struct(FIRST, LANES),
            struct(16 * PEER_ROWS, LANES),
            struct(PEER_ROWS, LANES),
            struct(PEER_ROWS, LANES),
        ),
        in_specs=[SMEM] * 3 + [VMEM] * 3,
        out_specs=(VMEM,) * 4,
        scratch_shapes=[cols4],
        name="first_density",
    )(send, ghost_lists, ghost_counts, table, ghosts, local_rho)

    ghost_rho = exchange(fine_rho, lower_rho, upper_rho)

    density, state = pl.pallas_call(
        rest_density_kernel,
        out_shape=(struct(blocks, LANES), struct(3, blocks, LANES)),
        in_specs=[SMEM] * 3 + [VMEM] * 5,
        out_specs=(VMEM,) * 2,
        scratch_shapes=[cols4],
        name="rest_density",
    )(ghost_lists, ghost_counts, live_blocks, table, ghosts, local_rho, first, energy2)

    cols10 = pltpu.VMEM((10, LANES, LANES), F32)
    acc5 = pltpu.VMEM((5, LANES, LANES), F32)
    local_force = pl.pallas_call(
        local_force_kernel,
        out_shape=struct(5, blocks, LANES),
        in_specs=[SMEM] * 3 + [VMEM] * 2,
        out_specs=VMEM,
        scratch_shapes=[cols10, acc5],
        name="local_force",
    )(local_lists, local_counts, live_blocks, table, state)

    forces, least = pl.pallas_call(
        ghost_force_kernel,
        out_shape=(struct(5, blocks, LANES), struct(1)),
        in_specs=[SMEM] * 3 + [VMEM] * 6,
        out_specs=(VMEM, SMEM),
        scratch_shapes=[pltpu.VMEM((3, 18 * PEER_ROWS, LANES), F32), cols10, acc5],
        name="ghost_force",
    )(
        ghost_lists,
        ghost_counts,
        live_blocks,
        table,
        state,
        ghosts,
        ghost_rho,
        smooth2,
        local_force,
    )

    timestep = lax.pmin(least, ("gx", "gy"))
    kick, heating = pl.pallas_call(
        scale_kernel,
        out_shape=(struct(3, blocks * LANES), struct(blocks, LANES)),
        in_specs=[SMEM, VMEM],
        out_specs=(VMEM,) * 2,
        name="scale",
    )(timestep, forces)
    return (density.reshape(-1), kick, heating.reshape(-1))


def solution(mesh):
    return jax.shard_map(
        shards,
        mesh=mesh,
        in_specs=(
            P(None, ("gx", "gy")),
            P(None, ("gx", "gy")),
            P(("gx", "gy")),
            P(("gx", "gy")),
            P(("gx", "gy")),
            P(("gx", "gy")),
            P(("gx", "gy"), None, None),
            P(("gx", "gy"), None),
            P(("gx", "gy")),
        ),
        out_specs=(P(("gx", "gy")), P(None, ("gx", "gy")), P(("gx", "gy"))),
        check_vma=False,
    )
```

```python
import math

import jax
import jax.numpy as jnp
from jax import lax
from jax.experimental import pallas as pl
from jax.experimental.pallas import tpu as pltpu
from jax.sharding import PartitionSpec as P

COURANT = 0.3
FAR_STEP = 1e30
TINY = 1e-30
LANES = 128
CHUNK = 8
FIRST = 24
PEER_TILES = 14
PEER_ROWS = 16
F32 = jnp.float32

SMEM = pl.BlockSpec(memory_space=pltpu.SMEM)
VMEM = pl.BlockSpec(memory_space=pltpu.VMEM)


def struct(*shape):
    return jax.ShapeDtypeStruct(shape, F32)


def columns(row):
    return jnp.broadcast_to(row, (LANES, LANES)).T


def spread(row):
    return jnp.broadcast_to(row, (CHUNK, LANES))


def pack_kernel(send, position, velocity, mass, smooth, energy, table, fine, lower, upper):
    blocks = mass.shape[0]

    def build(k, carry):
        at = pl.ds(pl.multiple_of(k * LANES, LANES), LANES)
        row = pl.ds(k, 1)
        table[k] = jnp.concatenate(
            [position[:, at], mass[row, :], -2.0 * velocity[:, at], smooth[row, :]], axis=0
        )
        return carry

    lax.fori_loop(0, blocks, build, 0)

    def fill(target, first_tile, p):
        for s in range(12):
            k = send[p * 12 + s]
            target[first_tile + s] = table[k]
            target[first_tile + 12 + s // 8, s % 8 : s % 8 + 1, :] = energy[pl.ds(k, 1), :]
        target[first_tile + 13, 4:8, :] = jnp.zeros((4, LANES), F32)

    def peer(p, carry):
        fill(fine, p * PEER_TILES, p)
        return carry

    lax.fori_loop(0, 16, peer, 0)
    fill(lower, 0, 16)
    fill(upper, 0, 17)


def over_blocks(order, lo, hi, prepare, gather, finish):
    @pl.when(hi > lo)
    def _():
        prepare(order[lo], 0)

        def pair(i, carry):
            for side in range(2):
                at = lo + 2 * i + side
                this = order[jnp.minimum(at, hi - 1)]
                after = order[jnp.minimum(at + 1, hi - 1)]
                before = order[jnp.minimum(jnp.maximum(at - 1, lo), hi - 1)]
                head, tail = gather(this, side)
                head()
                finish(before, 1 - side)
                prepare(after, 1 - side)
                tail()
            return carry

        lax.fori_loop(0, (hi - lo + 1) // 2, pair, 0)
        finish(order[hi - 1], 1)


def slots_of(lists, t, ghosts):
    def at(j):
        s = lists[j, t]
        if not ghosts:
            return s, s
        peer = (jnp.maximum(s - LANES, 0) * 171) >> 11
        return s + 2 * peer, s + 4 * peer

    return at


def head_and_tail(count, run):
    def head():
        run([0, 1, 2, 3], True)

    def tail():
        def two(i, carry):
            run([4 + 2 * i, 5 + 2 * i], False)
            return carry

        lax.fori_loop(0, (count - 4) // 2, two, 0)

        @pl.when(count % 2 == 1)
        def _():
            run([count - 1], False)

    return head, tail


def density_blocks(lists, counts, order, lo, hi, table, source, ghosts, out, cols, acc):
    def prepare(t, side):
        for f in range(3):
            cols[side][f] = columns(table[t, f : f + 1, :])
        h = table[t, 7:8, :]
        cols[side][3] = columns(0.25 / (h * h))

    def finish(t, side):
        h = table[t, 7:8, :]
        total = jnp.sum(acc[side][...].T, axis=0, keepdims=True)
        out[pl.ds(t, 1), :] = (21.0 / (4.0 * math.pi)) / (h * h * h) * total

    def gather(t, side):
        slot = slots_of(lists, t, ghosts)

        def run(js, first):
            tiles = [slot(j)[0] for j in js]
            rows = [[spread(source[k, f : f + 1, :]) for f in range(4)] for k in tiles]
            for c in range(LANES // CHUNK):
                at = pl.ds(c * CHUNK, CHUNK)
                xa, ya, za, scale = [cols[side][f, at, :] for f in range(4)]
                total = None if first else acc[side][at, :]
                for xs, ys, zs, ms in rows:
                    dx = xa - xs
                    dy = ya - ys
                    dz = za - zs
                    u2 = (dx * dx + dy * dy + dz * dz) * scale
                    u = u2 * lax.rsqrt(jnp.maximum(u2, TINY))
                    t1 = jnp.maximum(1.0 - u, 0.0)
                    t2 = t1 * t1
                    term = (t2 * ms) * (t2 * (1.25 - t1))
                    total = term if total is None else total + term
                acc[side][at, :] = total

        return head_and_tail(counts[t], run)

    over_blocks(order, lo, hi, prepare, gather, finish)


def pure_density_kernel(lists, counts, order, bounds, table, out, c0, c1, a0, a1):
    out[...] = jnp.zeros_like(out)
    density_blocks(
        lists, counts, order, 0, bounds[0], table, table, False, out, (c0, c1), (a0, a1)
    )


def first_density_kernel(
    send, lists, counts, order, bounds, table, source, rho, first, fine, lower, upper, c0, c1, a0, a1
):
    first[...] = rho[0:FIRST, :]
    density_blocks(
        lists, counts, order, bounds[0], bounds[1], table, source, True, first, (c0, c1), (a0, a1)
    )

    def fill(target, first_row, p):
        for s in range(12):
            target[pl.ds(first_row + s, 1), :] = first[pl.ds(send[p * 12 + s], 1), :]
        for s in range(12, 16):
            target[pl.ds(first_row + s, 1), :] = jnp.zeros((1, LANES), F32)

    def peer(p, carry):
        fill(fine, p * PEER_ROWS, p)
        return carry

    lax.fori_loop(0, 16, peer, 0)
    fill(lower, 0, 16)
    fill(upper, 0, 17)


def rest_density_kernel(
    lists, counts, order, bounds, table, source, rho, first, energy, density, state, c0, c1, a0, a1
):
    density[...] = rho[...]
    density[0:FIRST, :] = first[...]
    density_blocks(
        lists, counts, order, bounds[1], bounds[2], table, source, True, density, (c0, c1), (a0, a1)
    )
    thermal = energy[...]
    dens = density[...]
    state[0] = (2.0 / 3.0) * thermal / dens
    state[1] = jnp.sqrt((10.0 / 9.0) * thermal)
    state[2] = 4.0 * dens


def force_blocks(lists, counts, order, lo, hi, table, state, source, source_state, ghosts, out, cols, acc):
    def prepare(t, side):
        for i, f in enumerate((0, 1, 2, 4, 5, 6, 7)):
            cols[side][i] = columns(table[t, f : f + 1, :])
        for f in range(3):
            cols[side][7 + f] = columns(state[f, pl.ds(t, 1), :])

    def finish(t, side):
        at = pl.ds(t, 1)
        scale = 210.0 / math.pi
        for f in range(4):
            total = jnp.sum(acc[side][f].T, axis=0, keepdims=True)
            out[f, at, :] = (scale if f < 3 else 0.25 * scale) * total
        out[4, at, :] = 0.25 * jnp.max(acc[side][4].T, axis=0, keepdims=True)

    def gather(t, side):
        slot = slots_of(lists, t, ghosts)

        def run(js, first):
            slots = [slot(j) for j in js]
            for c in range(LANES // CHUNK):
                at = pl.ds(c * CHUNK, CHUNK)
                xa, ya, za, ua, va, wa, ha, pa, ca, ra = [cols[side][f, at, :] for f in range(10)]
                sums = None if first else [acc[side][f, at, :] for f in range(5)]
                for tile, row in slots:
                    xs, ys, zs, ms, us, vs, ws, hs = [
                        spread(source[tile, f : f + 1, :]) for f in range(8)
                    ]
                    ps, cs, rs = [spread(source_state[f, pl.ds(row, 1), :]) for f in range(3)]
                    dx = xa - xs
                    dy = ya - ys
                    dz = za - zs
                    r2 = dx * dx + dy * dy + dz * dz
                    w = dx * (ua - us) + dy * (va - vs) + dz * (wa - ws)
                    q = 1.0 / (ha + hs)
                    q2 = q * q
                    u2 = r2 * q2
                    u = u2 * lax.rsqrt(jnp.maximum(u2, TINY))
                    tq = jnp.maximum(1.0 - u, 0.0) * q
                    slope = (tq * tq) * (tq * q2)
                    m = (jnp.maximum(w, 0.0) * q) / (u2 + 0.0025)
                    visc = m * (ca + cs + m) / (ra + rs)
                    coef = (slope * ms) * (pa + ps + visc)
                    terms = [coef * dx, coef * dy, coef * dz, coef * w, m]
                    if sums is None:
                        sums = terms
                    else:
                        sums = [a + b for a, b in zip(sums[:4], terms[:4])] + [
                            jnp.maximum(sums[4], m)
                        ]
                for f in range(5):
                    acc[side][f, at, :] = sums[f]

        return head_and_tail(counts[t], run)

    over_blocks(order, lo, hi, prepare, gather, finish)


def pure_force_kernel(lists, counts, order, bounds, table, state, out, c0, c1, a0, a1):
    out[...] = jnp.zeros_like(out)
    force_blocks(
        lists, counts, order, 0, bounds[0], table, state, table, state, False, out, (c0, c1), (a0, a1)
    )


def mixed_force_kernel(
    lists, counts, order, bounds, table, state, source, ghost_rho, local, out, least, wide, c0, c1, a0, a1
):
    out[...] = local[...]
    blocks = table.shape[0]
    for f in range(3):
        wide[f, 0:blocks, :] = state[f]
    for p in range(18):
        at = pl.ds(blocks + p * PEER_ROWS, PEER_ROWS)
        tile = blocks + p * PEER_TILES + 12
        thermal = source[tile : tile + 2].reshape(PEER_ROWS, LANES)
        dens = ghost_rho[p * PEER_ROWS : (p + 1) * PEER_ROWS, :]
        wide[0, at, :] = (2.0 / 3.0) * thermal / dens
        wide[1, at, :] = jnp.sqrt((10.0 / 9.0) * thermal)
        wide[2, at, :] = 4.0 * dens
    force_blocks(
        lists, counts, order, bounds[0], bounds[2], table, state, source, wide, True, out, (c0, c1), (a0, a1)
    )
    sound = state[1]
    smooth = table[:, 7:8, :].reshape(blocks, LANES)
    step = COURANT * smooth / (sound + 1.2 * (sound + 2.0 * out[4]))
    index = lax.broadcasted_iota(jnp.int32, step.shape, 0)
    smallest = jnp.min(jnp.where(index < bounds[3], step, FAR_STEP))
    least[...] = jnp.full(least.shape, smallest, F32)


def scale_kernel(least, forces, kick, heating):
    dt = jnp.min(least[...])

    def block(k, carry):
        row = pl.ds(k, 1)
        at = pl.ds(pl.multiple_of(k * LANES, LANES), LANES)
        for f in range(3):
            kick[f : f + 1, at] = dt * forces[f, row, :]
        return carry

    lax.fori_loop(0, forces.shape[1], block, 0)
    heating[...] = dt * forces[3]


def block_order(nbr_list, nbr_count, live):
    blocks, width = nbr_list.shape
    k = jnp.arange(blocks, dtype=jnp.int32)
    used = jnp.arange(width, dtype=jnp.int32)[None, :] < nbr_count[:, None]
    mixed = jnp.any(used & (nbr_list >= blocks), axis=1)
    kind = jnp.where(mixed, jnp.where(k < FIRST, 1, 2), 0)
    kind = jnp.where(k < live, kind, 3)
    key = kind * blocks + k
    rank = jnp.sum((key[None, :] < key[:, None]).astype(jnp.int32), axis=1)
    order = jnp.sum(jnp.where(rank[None, :] == k[:, None], k[None, :], 0), axis=1)
    bounds = jnp.sum((kind[None, :] <= jnp.arange(3, dtype=jnp.int32)[:, None]).astype(jnp.int32), axis=1)
    return order, jnp.concatenate([bounds, live])


def shards(
    position, velocity, mass, smoothing, energy, live_blocks, send_list, nbr_list, nbr_count
):
    blocks = nbr_count.shape[0]
    mass2 = mass.reshape(blocks, LANES)
    smooth2 = smoothing.reshape(blocks, LANES)
    energy2 = energy.reshape(blocks, LANES)
    send = send_list.reshape(-1)

    table, fine, lower, upper = pl.pallas_call(
        pack_kernel,
        out_shape=(
            struct(blocks, 8, LANES),
            struct(16 * PEER_TILES, 8, LANES),
            struct(PEER_TILES, 8, LANES),
            struct(PEER_TILES, 8, LANES),
        ),
        in_specs=[SMEM] + [VMEM] * 5,
        out_specs=(VMEM,) * 4,
        name="pack",
    )(send, position, velocity, mass2, smooth2, energy2)

    def exchange(fine, lower, upper):
        shape = (16, fine.shape[0] // 16) + fine.shape[1:]
        arrived = lax.all_to_all(fine.reshape(shape), "gy", split_axis=0, concat_axis=0, tiled=True)
        size = lax.axis_size("gx")
        up = [(i, i + 1) for i in range(size - 1)]
        down = [(j, i) for i, j in up]
        before = lax.ppermute(upper, "gx", up)
        after = lax.ppermute(lower, "gx", down)
        return jnp.concatenate([arrived.reshape(fine.shape), before, after], axis=0)

    ghosts = exchange(fine, lower, upper)
    source = jnp.concatenate([table, ghosts], axis=0)
    lists = nbr_list.T
    order, bounds = block_order(nbr_list, nbr_count, live_blocks)

    small = [pltpu.VMEM((4, LANES, LANES), F32)] * 2 + [pltpu.VMEM((LANES, LANES), F32)] * 2
    large = [pltpu.VMEM((10, LANES, LANES), F32)] * 2 + [pltpu.VMEM((5, LANES, LANES), F32)] * 2
    pure_rho = pl.pallas_call(
        pure_density_kernel,
        out_shape=struct(blocks, LANES),
        in_specs=[SMEM] * 4 + [VMEM],
        out_specs=VMEM,
        scratch_shapes=small,
        name="pure_density",
    )(lists, nbr_count, order, bounds, table)

    first, fine_rho, lower_rho, upper_rho = pl.pallas_call(
        first_density_kernel,
        out_shape=(
            struct(FIRST, LANES),
            struct(16 * PEER_ROWS, LANES),
            struct(PEER_ROWS, LANES),
            struct(PEER_ROWS, LANES),
        ),
        in_specs=[SMEM] * 5 + [VMEM] * 3,
        out_specs=(VMEM,) * 4,
        scratch_shapes=small,
        name="first_density",
    )(send, lists, nbr_count, order, bounds, table, source, pure_rho)

    ghost_rho = exchange(fine_rho, lower_rho, upper_rho)

    density, state = pl.pallas_call(
        rest_density_kernel,
        out_shape=(struct(blocks, LANES), struct(3, blocks, LANES)),
        in_specs=[SMEM] * 4 + [VMEM] * 5,
        out_specs=(VMEM,) * 2,
        scratch_shapes=small,
        name="rest_density",
    )(lists, nbr_count, order, bounds, table, source, pure_rho, first, energy2)

    pure_force = pl.pallas_call(
        pure_force_kernel,
        out_shape=struct(5, blocks, LANES),
        in_specs=[SMEM] * 4 + [VMEM] * 2,
        out_specs=VMEM,
        scratch_shapes=large,
        name="pure_force",
    )(lists, nbr_count, order, bounds, table, state)

    devices = lax.axis_size("gx") * lax.axis_size("gy")
    forces, least = pl.pallas_call(
        mixed_force_kernel,
        out_shape=(struct(5, blocks, LANES), struct(devices, LANES)),
        in_specs=[SMEM] * 4 + [VMEM] * 5,
        out_specs=(VMEM,) * 2,
        scratch_shapes=[pltpu.VMEM((3, blocks + 18 * PEER_ROWS, LANES), F32)] + large,
        name="mixed_force",
    )(lists, nbr_count, order, bounds, table, state, source, ghost_rho, pure_force)

    steps = lax.all_to_all(
        least.reshape(devices, 1, LANES), ("gx", "gy"), split_axis=0, concat_axis=0, tiled=True
    )
    kick, heating = pl.pallas_call(
        scale_kernel,
        out_shape=(struct(3, blocks * LANES), struct(blocks, LANES)),
        in_specs=[VMEM] * 2,
        out_specs=(VMEM,) * 2,
        name="scale",
    )(steps.reshape(devices, LANES), forces)
    return (density.reshape(-1), kick, heating.reshape(-1))


def solution(mesh):
    return jax.shard_map(
        shards,
        mesh=mesh,
        in_specs=(
            P(None, ("gx", "gy")),
            P(None, ("gx", "gy")),
            P(("gx", "gy")),
            P(("gx", "gy")),
            P(("gx", "gy")),
            P(("gx", "gy")),
            P(("gx", "gy"), None, None),
            P(("gx", "gy"), None),
            P(("gx", "gy")),
        ),
        out_specs=(P(("gx", "gy")), P(None, ("gx", "gy")), P(("gx", "gy"))),
        check_vma=False,
    )
```

```python
import functools
import math

import jax
import jax.numpy as jnp
from jax import lax
from jax.experimental import pallas as pl
from jax.experimental.pallas import tpu as pltpu
from jax.sharding import PartitionSpec as P

COURANT = 0.3
FAR_STEP = 1e30
TINY = 1e-30
LANES = 128
CHUNK = 8
FIRST = 24
PEER_TILES = 14
PEER_ROWS = 16
F32 = jnp.float32

SMEM = pl.BlockSpec(memory_space=pltpu.SMEM)
VMEM = pl.BlockSpec(memory_space=pltpu.VMEM)


def struct(*shape):
    return jax.ShapeDtypeStruct(shape, F32)


def columns(row):
    return jnp.broadcast_to(row, (LANES, LANES)).T


def spread(row):
    return jnp.broadcast_to(row, (CHUNK, LANES))


def block_order(lists, counts, live):
    width, blocks = lists.shape
    k = lax.broadcasted_iota(jnp.int32, (1, blocks), 1)
    used = lax.broadcasted_iota(jnp.int32, lists.shape, 0) < counts
    mixed = jnp.max(jnp.where(used & (lists >= blocks), 1.0, 0.0), axis=0, keepdims=True) > 0.0
    kind = jnp.where(mixed, jnp.where(k < FIRST, 1, 2), 0)
    kind = jnp.where(k < live, kind, 3)
    key = (kind * blocks + k).astype(F32)
    key_column = jnp.broadcast_to(key, (blocks, blocks)).T
    rank = jnp.sum(jnp.where(key_column < key, 1.0, 0.0), axis=0, keepdims=True)
    rank_column = jnp.broadcast_to(rank, (blocks, blocks)).T
    sublane = lax.broadcasted_iota(jnp.int32, (blocks, blocks), 0).astype(F32)
    hit = rank_column == k.astype(F32)
    order = jnp.sum(jnp.where(hit, sublane, 0.0), axis=0, keepdims=True).astype(jnp.int32)
    ends = jnp.full((1, blocks), live, jnp.int32)
    for c in range(3):
        end = jnp.sum(jnp.where(kind <= c, 1.0, 0.0), axis=1, keepdims=True).astype(jnp.int32)
        ends = jnp.where(k == c, end, ends)
    return order, ends


def pack_kernel(
    send, live, lists, counts, position, velocity, mass, smooth, energy, table, fine, lower, upper, order, bounds
):
    blocks = mass.shape[0]

    def build(k, carry):
        at = pl.ds(pl.multiple_of(k * LANES, LANES), LANES)
        row = pl.ds(k, 1)
        table[k] = jnp.concatenate(
            [position[:, at], mass[row, :], -2.0 * velocity[:, at], smooth[row, :]], axis=0
        )
        return carry

    lax.fori_loop(0, blocks, build, 0)

    def fill(target, first_tile, p):
        for s in range(12):
            k = send[s, 0, p]
            target[first_tile + s] = table[k]
            target[first_tile + 12 + s // 8, s % 8 : s % 8 + 1, :] = energy[pl.ds(k, 1), :]
        target[first_tile + 13, 4:8, :] = jnp.zeros((4, LANES), F32)

    def peer(p, carry):
        fill(fine, p * PEER_TILES, p)
        return carry

    lax.fori_loop(0, 16, peer, 0)
    fill(lower, 0, 16)
    fill(upper, 0, 17)
    order[...], bounds[...] = block_order(lists[...], counts[...], live[0])


def over_blocks(order, lo, hi, prepare, gather, finish):
    @pl.when(hi > lo)
    def _():
        for step in prepare(order[lo], 0):
            step()

        def one(at, side):
            this = order[at]
            after = order[jnp.minimum(at + 1, hi - 1)]
            before = order[jnp.maximum(at - 1, lo)]
            gather(this, side, finish(before, 1 - side), prepare(after, 1 - side))

        def pair(i, carry):
            at = lo + 2 * i
            one(at, 0)

            @pl.when(at + 1 < hi)
            def _():
                one(at + 1, 1)

            return carry

        lax.fori_loop(0, (hi - lo + 1) // 2, pair, 0)
        for side in range(2):

            @pl.when((hi - lo - 1) % 2 == side)
            def _():
                for step in finish(order[hi - 1], side):
                    step()


def slots_of(lists, t, ghosts):
    def at(j):
        s = lists[j, t]
        if not ghosts:
            return s, s
        peer = (jnp.maximum(s - LANES, 0) * 171) >> 11
        return s + 2 * peer, s + 4 * peer

    return at


def gather_all(count, run, folds, makes):
    run([0, 1], True, folds)

    @pl.when(count > 3)
    def _():
        run([2, 3], False, makes)

    def two(i, carry):
        run([4 + 2 * i, 5 + 2 * i], False, [])
        return carry

    lax.fori_loop(0, (count - 4) // 2, two, 0)

    @pl.when(count % 2 == 1)
    def _():
        run([count - 1], False, [])


def between(steps, c):
    chunks = LANES // CHUNK
    for step in steps[c * len(steps) // chunks : (c + 1) * len(steps) // chunks]:
        step()


def density_blocks(lists, counts, order, lo, hi, table, source, ghosts, out, cols, acc):
    def prepare(t, side):
        def make(f):
            h = table[t, 7:8, :]
            cols[side][f] = columns(table[t, f : f + 1, :] if f < 3 else 0.25 / (h * h))

        return [functools.partial(make, f) for f in range(4)]

    def finish(t, side):
        def fold():
            h = table[t, 7:8, :]
            total = jnp.sum(acc[side][...].T, axis=0, keepdims=True)
            out[pl.ds(t, 1), :] = (21.0 / (4.0 * math.pi)) / (h * h * h) * total

        return [fold]

    def gather(t, side, folds, makes):
        slot = slots_of(lists, t, ghosts)

        def run(js, first, steps):
            tiles = [slot(j)[0] for j in js]
            rows = [[spread(source[k, f : f + 1, :]) for f in range(4)] for k in tiles]
            for c in range(LANES // CHUNK):
                at = pl.ds(c * CHUNK, CHUNK)
                xa, ya, za, scale = [cols[side][f, at, :] for f in range(4)]
                total = None if first else acc[side][at, :]
                for xs, ys, zs, ms in rows:
                    dx = xa - xs
                    dy = ya - ys
                    dz = za - zs
                    u2 = (dx * dx + dy * dy + dz * dz) * scale
                    u = u2 * lax.rsqrt(jnp.maximum(u2, TINY))
                    t1 = jnp.maximum(1.0 - u, 0.0)
                    t2 = t1 * t1
                    term = (t2 * ms) * (t2 * (1.25 - t1))
                    total = term if total is None else total + term
                acc[side][at, :] = total
                between(steps, c)

        gather_all(counts[t], run, folds, makes)

    over_blocks(order, lo, hi, prepare, gather, finish)


def pure_density_kernel(lists, counts, order, bounds, table, out, c0, c1, a0, a1):
    out[...] = jnp.zeros_like(out)
    density_blocks(
        lists, counts, order, 0, bounds[0], table, table, False, out, (c0, c1), (a0, a1)
    )


def first_density_kernel(
    send, lists, counts, order, bounds, table, source, rho, first, fine, lower, upper, c0, c1, a0, a1
):
    first[...] = rho[0:FIRST, :]
    density_blocks(
        lists, counts, order, bounds[0], bounds[1], table, source, True, first, (c0, c1), (a0, a1)
    )

    def fill(target, first_row, p):
        for s in range(12):
            target[pl.ds(first_row + s, 1), :] = first[pl.ds(send[s, 0, p], 1), :]
        for s in range(12, 16):
            target[pl.ds(first_row + s, 1), :] = jnp.zeros((1, LANES), F32)

    def peer(p, carry):
        fill(fine, p * PEER_ROWS, p)
        return carry

    lax.fori_loop(0, 16, peer, 0)
    fill(lower, 0, 16)
    fill(upper, 0, 17)


def rest_density_kernel(
    lists, counts, order, bounds, table, source, rho, first, energy, density, state, c0, c1, a0, a1
):
    density[...] = rho[...]
    density[0:FIRST, :] = first[...]
    density_blocks(
        lists, counts, order, bounds[1], bounds[2], table, source, True, density, (c0, c1), (a0, a1)
    )
    thermal = energy[...]
    dens = density[...]
    state[0] = (2.0 / 3.0) * thermal / dens
    state[1] = jnp.sqrt((10.0 / 9.0) * thermal)
    state[2] = 4.0 * dens


def force_blocks(lists, counts, order, lo, hi, table, state, source, source_state, ghosts, out, rest, cols, acc):
    def prepare(t, side):
        def make(i):
            if i < 7:
                f = (0, 1, 2, 4, 5, 6, 7)[i]
                cols[side][i] = columns(table[t, f : f + 1, :])
            else:
                cols[side][i] = columns(state[i - 7, pl.ds(t, 1), :])

        return [functools.partial(make, i) for i in range(10)]

    def finish(t, side):
        at = pl.ds(t, 1)
        scale = 210.0 / math.pi

        def fold(f):
            if f < 3:
                lanes = pl.ds(pl.multiple_of(t * LANES, LANES), LANES)
                out[f : f + 1, lanes] = scale * jnp.sum(acc[side][f].T, axis=0, keepdims=True)
            elif f == 3:
                rest[0, at, :] = 0.25 * scale * jnp.sum(acc[side][3].T, axis=0, keepdims=True)
            else:
                rest[1, at, :] = 0.25 * jnp.max(acc[side][4].T, axis=0, keepdims=True)

        return [functools.partial(fold, f) for f in range(5)]

    def gather(t, side, folds, makes):
        slot = slots_of(lists, t, ghosts)

        def run(js, first, steps):
            slots = [slot(j) for j in js]
            for c in range(LANES // CHUNK):
                at = pl.ds(c * CHUNK, CHUNK)
                xa, ya, za, ua, va, wa, ha, pa, ca, ra = [cols[side][f, at, :] for f in range(10)]
                sums = None if first else [acc[side][f, at, :] for f in range(5)]
                for tile, row in slots:
                    xs, ys, zs, ms, us, vs, ws, hs = [
                        spread(source[tile, f : f + 1, :]) for f in range(8)
                    ]
                    ps, cs, rs = [spread(source_state[f, pl.ds(row, 1), :]) for f in range(3)]
                    dx = xa - xs
                    dy = ya - ys
                    dz = za - zs
                    r2 = dx * dx + dy * dy + dz * dz
                    w = dx * (ua - us) + dy * (va - vs) + dz * (wa - ws)
                    q = 1.0 / (ha + hs)
                    q2 = q * q
                    u2 = r2 * q2
                    u = u2 * lax.rsqrt(jnp.maximum(u2, TINY))
                    tq = jnp.maximum(1.0 - u, 0.0) * q
                    slope = (tq * tq) * (tq * q2)
                    m = (jnp.maximum(w, 0.0) * q) / (u2 + 0.0025)
                    visc = m * (ca + cs + m) / (ra + rs)
                    coef = (slope * ms) * (pa + ps + visc)
                    terms = [coef * dx, coef * dy, coef * dz, coef * w, m]
                    if sums is None:
                        sums = terms
                    else:
                        sums = [a + b for a, b in zip(sums[:4], terms[:4])] + [
                            jnp.maximum(sums[4], m)
                        ]
                for f in range(5):
                    acc[side][f, at, :] = sums[f]
                between(steps, c)

        gather_all(counts[t], run, folds, makes)

    over_blocks(order, lo, hi, prepare, gather, finish)


def pure_force_kernel(lists, counts, order, bounds, table, state, out, rest, c0, c1, a0, a1):
    out[...] = jnp.zeros_like(out)
    rest[...] = jnp.zeros_like(rest)
    force_blocks(
        lists, counts, order, 0, bounds[0], table, state, table, state, False, out, rest,
        (c0, c1), (a0, a1)
    )


def mixed_force_kernel(
    lists, counts, order, bounds, table, state, source, rho, rho_before, rho_after,
    local, local_rest, out, rest, least, wide, c0, c1, a0, a1
):
    out[...] = local[...]
    rest[...] = local_rest[...]
    blocks = table.shape[0]
    for f in range(3):
        wide[f, 0:blocks, :] = state[f]
    for p in range(18):
        at = pl.ds(blocks + p * PEER_ROWS, PEER_ROWS)
        tile = blocks + p * PEER_TILES + 12
        thermal = source[tile : tile + 2].reshape(PEER_ROWS, LANES)
        if p < 16:
            dens = rho[p * PEER_ROWS : (p + 1) * PEER_ROWS, :]
        else:
            dens = (rho_before if p == 16 else rho_after)[...]
        wide[0, at, :] = (2.0 / 3.0) * thermal / dens
        wide[1, at, :] = jnp.sqrt((10.0 / 9.0) * thermal)
        wide[2, at, :] = 4.0 * dens
    force_blocks(
        lists, counts, order, bounds[0], bounds[2], table, state, source, wide, True, out, rest,
        (c0, c1), (a0, a1)
    )
    sound = state[1]
    smooth = table[:, 7:8, :].reshape(blocks, LANES)
    step = COURANT * smooth / (sound + 1.2 * (sound + 2.0 * rest[1]))
    index = lax.broadcasted_iota(jnp.int32, step.shape, 0)
    smallest = jnp.min(jnp.where(index < bounds[3], step, FAR_STEP))
    least[...] = jnp.full(least.shape, smallest, F32)


def scale_kernel(least, forces, rest, kick, heating):
    dt = jnp.min(least[...])
    kick[...] = dt * forces[...]
    heating[...] = dt * rest[0]


def shards(
    position, velocity, mass, smoothing, energy, live_blocks, send_list, nbr_list, nbr_count
):
    blocks = nbr_count.shape[0]
    mass2 = mass.reshape(blocks, LANES)
    smooth2 = smoothing.reshape(blocks, LANES)
    energy2 = energy.reshape(blocks, LANES)
    send = jnp.transpose(send_list, (2, 0, 1))
    lists = nbr_list.T

    table, fine, lower, upper, order, bounds = pl.pallas_call(
        pack_kernel,
        out_shape=(
            struct(blocks, 8, LANES),
            struct(16 * PEER_TILES, 8, LANES),
            struct(PEER_TILES, 8, LANES),
            struct(PEER_TILES, 8, LANES),
            jax.ShapeDtypeStruct((1, blocks), jnp.int32),
            jax.ShapeDtypeStruct((1, blocks), jnp.int32),
        ),
        in_specs=[SMEM] * 2 + [VMEM] * 7,
        out_specs=(VMEM,) * 6,
        name="pack",
    )(
        send,
        live_blocks,
        lists,
        nbr_count.reshape(1, blocks),
        position,
        velocity,
        mass2,
        smooth2,
        energy2,
    )
    order = order.reshape(-1)
    bounds = bounds.reshape(-1)

    def exchange(fine, lower, upper):
        shape = (16, fine.shape[0] // 16) + fine.shape[1:]
        arrived = lax.all_to_all(fine.reshape(shape), "gy", split_axis=0, concat_axis=0, tiled=True)
        size = lax.axis_size("gx")
        up = [(i, i + 1) for i in range(size - 1)]
        down = [(j, i) for i, j in up]
        before = lax.ppermute(upper, "gx", up)
        after = lax.ppermute(lower, "gx", down)
        return arrived.reshape(fine.shape), before, after

    ghosts = exchange(fine, lower, upper)
    source = jnp.concatenate([table, *ghosts], axis=0)

    small = [pltpu.VMEM((4, LANES, LANES), F32)] * 2 + [pltpu.VMEM((LANES, LANES), F32)] * 2
    large = [pltpu.VMEM((10, LANES, LANES), F32)] * 2 + [pltpu.VMEM((5, LANES, LANES), F32)] * 2
    pure_rho = pl.pallas_call(
        pure_density_kernel,
        out_shape=struct(blocks, LANES),
        in_specs=[SMEM] * 4 + [VMEM],
        out_specs=VMEM,
        scratch_shapes=small,
        name="pure_density",
    )(lists, nbr_count, order, bounds, table)

    first, fine_rho, lower_rho, upper_rho = pl.pallas_call(
        first_density_kernel,
        out_shape=(
            struct(FIRST, LANES),
            struct(16 * PEER_ROWS, LANES),
            struct(PEER_ROWS, LANES),
            struct(PEER_ROWS, LANES),
        ),
        in_specs=[SMEM] * 5 + [VMEM] * 3,
        out_specs=(VMEM,) * 4,
        scratch_shapes=small,
        name="first_density",
    )(send, lists, nbr_count, order, bounds, table, source, pure_rho)

    ghost_rho = exchange(fine_rho, lower_rho, upper_rho)

    density, state = pl.pallas_call(
        rest_density_kernel,
        out_shape=(struct(blocks, LANES), struct(3, blocks, LANES)),
        in_specs=[SMEM] * 4 + [VMEM] * 5,
        out_specs=(VMEM,) * 2,
        scratch_shapes=small,
        name="rest_density",
    )(lists, nbr_count, order, bounds, table, source, pure_rho, first, energy2)

    pure_force = pl.pallas_call(
        pure_force_kernel,
        out_shape=(struct(3, blocks * LANES), struct(2, blocks, LANES)),
        in_specs=[SMEM] * 4 + [VMEM] * 2,
        out_specs=(VMEM,) * 2,
        scratch_shapes=large,
        name="pure_force",
    )(lists, nbr_count, order, bounds, table, state)

    devices = lax.axis_size("gx") * lax.axis_size("gy")
    forces, rest, least = pl.pallas_call(
        mixed_force_kernel,
        out_shape=(struct(3, blocks * LANES), struct(2, blocks, LANES), struct(devices, LANES)),
        in_specs=[SMEM] * 4 + [VMEM] * 8,
        out_specs=(VMEM,) * 3,
        scratch_shapes=[pltpu.VMEM((3, blocks + 18 * PEER_ROWS, LANES), F32)] + large,
        name="mixed_force",
    )(lists, nbr_count, order, bounds, table, state, source, *ghost_rho, *pure_force)

    steps = lax.all_to_all(
        least.reshape(devices, 1, LANES), ("gx", "gy"), split_axis=0, concat_axis=0, tiled=True
    )
    kick, heating = pl.pallas_call(
        scale_kernel,
        out_shape=(struct(3, blocks * LANES), struct(blocks, LANES)),
        in_specs=[VMEM] * 3,
        out_specs=(VMEM,) * 2,
        name="scale",
    )(steps.reshape(devices, LANES), forces, rest)
    return (density.reshape(-1), kick, heating.reshape(-1))


def solution(mesh):
    return jax.shard_map(
        shards,
        mesh=mesh,
        in_specs=(
            P(None, ("gx", "gy")),
            P(None, ("gx", "gy")),
            P(("gx", "gy")),
            P(("gx", "gy")),
            P(("gx", "gy")),
            P(("gx", "gy")),
            P(("gx", "gy"), None, None),
            P(("gx", "gy"), None),
            P(("gx", "gy")),
        ),
        out_specs=(P(("gx", "gy")), P(None, ("gx", "gy")), P(("gx", "gy"))),
        check_vma=False,
    )
```
